32 devices in a mesh: groups: 2 (over x), pts: 16 (over z, y, core).
Axes of the slice: x: 2, y: 2, z: 4, core: 2. Of those that a mesh axis runs over, the one named last changes fastest.
Arguments:
- points: bfloat16 [8192, 512], P(('groups', 'pts')), parts along dimension 0, may hold values from -6 to 6
- labels: int32 [8192], P(('groups', 'pts')), parts along dimension 0, may hold values from 0 to 15
- centres: bfloat16 [32768, 512], P(('groups', 'pts')), parts along dimension 0, may hold values from -6 to 6
- tri_inverse: bfloat16 [32768, 16384], P(('groups', 'pts')), parts along dimension 0, as said below
- beta: bfloat16 [32768, 16], P(('groups', 'pts')), parts along dimension 0, may hold values from -0.01171875 to 0.01171875
- bias: float32 [32], P('groups'), parts along dimension 0, may hold values from -3.2 to -2.2
Outputs:
- gradient: float32 [32768, 16], P(('groups', 'pts')), parts along dimension 0
- logits: float32 [8192, 16], P(('groups', 'pts')), parts along dimension 0
The draws below stay inside these ranges and needn't reach their ends.
There are 2 independent parts, one for each index of `groups`. The reference program is written for one: setup_inputs(seed, part) draws one part's arguments, and reference() takes and returns one part's arrays. A program takes and returns all parts, laid end to end along the dimension named above; each array names one. Nothing has to cross between parts.
Inputs may be any that keep to these rules, and one draw needn't show every extreme that they name: `tri_inverse`: upper triangular: entries below the diagonal are zero; the diagonal lies between 0.6 and 1.4.
All inputs are finite; a program needn't handle non-finite values.
Results may differ from the reference program's by a relative error of at most 0.0039.
Values may be sent and summed in bfloat16 or wider, within the bound.
A program may use at most 128 MiB of HBM per device.

```python
import math
import jax
import jax.numpy as jnp
from jax import lax

CENTRES = 16384
FEATURES = 512
CLASSES = 16
POINTS = 4096


def draw_tri_inverse(key, part):
    key_off, key_diag = jax.random.split(jax.random.fold_in(key, 7))
    offdiag = jax.random.normal(key_off, (CENTRES, CENTRES), jnp.float32) * (0.5 * CENTRES ** (-0.5))
    diagonal = jax.random.uniform(key_diag, (CENTRES,), jnp.float32, 0.6, 1.4)
    row_index = jnp.arange(CENTRES)[:, None]
    col_index = jnp.arange(CENTRES)[None, :]
    result = jnp.where(col_index > row_index, offdiag, 0.0)
    result = jnp.where(col_index == row_index, diagonal[:, None], result)
    return result.astype(jnp.bfloat16)


def place_ends(drawn, stream_key, least, high):
    spot = [jax.random.randint(jax.random.fold_in(stream_key, axis), (), 0, length) for axis, length in enumerate(drawn.shape)]
    main_axis = drawn.shape.index(max(drawn.shape))
    beside = spot[:main_axis] + [(spot[main_axis] + 1) % drawn.shape[main_axis]] + spot[main_axis + 1:]
    return drawn.at[tuple(spot)].set(least).at[tuple(beside)].set(high)


def steps_of(key, shape, shards, low, largest):
    loudness = 1.0
    for axis_at, blocks in shards:
        draws = jax.random.uniform(jax.random.fold_in(jax.random.fold_in(key, 6), axis_at), (blocks,), jnp.float32, low / len(shards), largest / len(shards))
        loudness = loudness * jnp.repeat(jnp.exp(draws), shape[axis_at] // blocks).reshape((-1,) + (1,) * (len(shape) - 1 - axis_at))
    return loudness


def scatter_about(rng, dims, spread, bound, cuts=(), held_as=jnp.bfloat16):
    values = spread * jax.random.normal(rng, dims, jnp.float32)
    if cuts:
        values = values * steps_of(rng, dims, cuts, -0.22, 0.18)
    return jnp.clip(values, -bound, bound).astype(held_as)


def setup_inputs(seed: int = 0, part: int = 0) -> dict:
    key_list = jax.random.split(jax.random.key(seed), 7)
    part_splits = jax.random.split(jax.random.fold_in(key_list[6], part), 7)
    return {
        "points": scatter_about(part_splits[0], (POINTS, FEATURES), 1.0, 6.0, ((0, 16),)),
        "labels": place_ends(jax.random.randint(part_splits[1], (POINTS,), 0, CLASSES), jax.random.fold_in(part_splits[1], 1), 0, CLASSES - 1).astype(jnp.int32),
        "centres": scatter_about(part_splits[2], (CENTRES, FEATURES), 1.0, 6.0, ((0, 16),)),
        "tri_inverse": draw_tri_inverse(jax.random.fold_in(jax.random.fold_in(key_list[6], part), 71), part),
        "beta": scatter_about(part_splits[4], (CENTRES, CLASSES), (16 * CENTRES) ** -0.5, 0.01171875, ((0, 16),)),
        "bias": jnp.clip(jax.random.uniform(part_splits[5], (CLASSES,), jnp.float32, -3.2, -2.2), -3.2, -2.2),
    }


def cube_kernel(point_block, centre_all):
    inner = jnp.dot(point_block, centre_all.T, preferred_element_type=jnp.float32)
    factor = 1.0 / math.sqrt(FEATURES)
    return ((inner * factor + 1.0) ** 3).astype(jnp.bfloat16)

def reference(points, labels, centres, tri_inverse, beta, bias):
    alpha = jnp.dot(tri_inverse, beta, preferred_element_type=jnp.float32).astype(jnp.bfloat16)
    block_size = math.gcd(POINTS, 1024)
    block_count = POINTS // block_size
    point_blocks = points.reshape(block_count, block_size, FEATURES)
    label_blocks = labels.reshape(block_count, block_size)
    classes_row = jnp.arange(CLASSES, dtype=jnp.int32)

    def advance(running, inputs):
        point_block, label_block = inputs
        kernel_tile = cube_kernel(point_block, centres)
        block_logits = jnp.dot(kernel_tile, alpha, preferred_element_type=jnp.float32) + bias[None, :]
        onehot = (label_block[:, None] == classes_row[None, :]).astype(jnp.float32)
        resid = (jax.nn.sigmoid(block_logits) - onehot).astype(jnp.bfloat16)
        update = lax.dot_general(kernel_tile, resid, (((0,), (0,)), ((), ())), preferred_element_type=jnp.float32)
        return (running + update, block_logits)
    grad_sum, logit_blocks = lax.scan(advance, jnp.zeros((CENTRES, CLASSES), jnp.float32), (point_blocks, label_blocks))
    grad_kernel = (grad_sum * (1.0 / math.sqrt(POINTS))).astype(jnp.bfloat16)
    gradient = lax.dot_general(tri_inverse, grad_kernel, (((0,), (0,)), ((), ())), preferred_element_type=jnp.float32)
    return (gradient, logit_blocks.reshape(POINTS, CLASSES))
```

```python
import math

import jax
import jax.numpy as jnp
from jax import lax
from jax.sharding import PartitionSpec as P


def cube_kernel(point_block, centre_block):
    inner = lax.dot_general(
        point_block, centre_block, (((1,), (1,)), ((), ())), preferred_element_type=jnp.float32
    )
    factor = 1.0 / math.sqrt(point_block.shape[1])
    return ((inner * factor + 1.0) ** 3).astype(jnp.bfloat16)


def on_device(points, labels, centres, tri_inverse, beta, bias):
    local_points = points.shape[0]
    local_centres = centres.shape[0]
    class_count = beta.shape[1]
    packing = 128 // class_count
    dense_centres = local_centres // packing
    total_points = local_points * lax.axis_size("pts")
    beta_dense = beta.reshape(dense_centres, 128)
    beta_part = lax.all_gather(beta_dense, "pts", axis=0, tiled=True)
    narrow = beta_part.reshape(beta_part.shape[0] * packing, class_count)
    columns = tri_inverse
    alpha_sum = jnp.dot(columns, narrow, preferred_element_type=jnp.float32)
    alpha_local = alpha_sum.astype(jnp.bfloat16)
    classes_row = jnp.arange(class_count, dtype=jnp.int32)
    onehot = (labels[:, None] == classes_row[None, :]).astype(jnp.float32)
    points_all = lax.all_gather(points, "pts", axis=0, tiled=True)
    kernel_tile = cube_kernel(points_all, centres)
    logit_part = jnp.dot(kernel_tile, alpha_local, preferred_element_type=jnp.float32)
    logit_dense = lax.psum_scatter(
        logit_part.reshape(total_points // packing, 128), "pts", scatter_dimension=0, tiled=True
    )
    logits = logit_dense.reshape(local_points, class_count) + bias[None, :]
    resid = (jax.nn.sigmoid(logits) - onehot).astype(jnp.bfloat16)
    resid_dense = resid.reshape(local_points // packing, 128)
    resid_all = lax.all_gather(resid_dense, "pts", axis=0, tiled=True)
    narrow = resid_all.reshape(total_points, class_count)
    grad_sum = lax.dot_general(
        kernel_tile, narrow, (((0,), (0,)), ((), ())), preferred_element_type=jnp.float32
    )
    grad_dense = grad_sum.reshape(dense_centres, 128)
    grad_kernel = (
        grad_dense.reshape(local_centres, class_count) * (1.0 / math.sqrt(total_points))
    ).astype(jnp.bfloat16)
    columns = tri_inverse
    term = lax.dot_general(
        columns, grad_kernel, (((0,), (0,)), ((), ())), preferred_element_type=jnp.float32
    )
    gradient_dense = lax.psum_scatter(
        term.reshape(lax.axis_size("pts") * dense_centres, 128),
        "pts",
        scatter_dimension=0,
        tiled=True,
    )
    return (gradient_dense.reshape(local_centres, class_count), logits)


def solution(mesh):
    return jax.shard_map(
        on_device,
        mesh=mesh,
        in_specs=(
            P(("groups", "pts"), None),
            P(("groups", "pts")),
            P(("groups", "pts"), None),
            P(("groups", "pts"), None),
            P(("groups", "pts"), None),
            P("groups"),
        ),
        out_specs=(P(("groups", "pts"), None), P(("groups", "pts"), None)),
        check_vma=False,
    )
```

```python
import functools
import math

import jax
import jax.numpy as jnp
from jax import lax
from jax.experimental import pallas as pl
from jax.experimental.pallas import tpu as pltpu
from jax.sharding import PartitionSpec as P

NT = (((1,), (1,)), ((), ()))
NN = (((1,), (0,)), ((), ()))


def dot(left, right, dims):
    return lax.dot_general(left, right, dims, preferred_element_type=jnp.float32)


def body(
    n, points, labels, centres, tri, beta, bias, grad_out, logits_out,
    tbuf, pbuf, cbuf, kbuf, bbuf, abuf, asum, lsend, lrecv, rbuf, gsend, grecv, tsend, trecv, total,
    t_sem, own_sem, b_send, b_recv, f_send, p_send, p_recv, c_send, c_recv, a_send, a_recv,
    l_send, l_recv, r_send, r_recv, g_send, g_recv, ts_sem, tr_sem,
):
    chips = n // 2
    depth = chips // 2
    me = lax.axis_index("pts")
    core = lax.rem(me, 2)
    chip = me // 2
    side = lax.rem(chip, 2)
    level = chip // 2
    partner = me + 1 - 2 * core
    size = centres.shape[0]
    factor = 1.0 / math.sqrt(points.shape[1])
    total_points = n * points.shape[0]
    classes = beta.shape[0]

    def remote(src, dst, send, recv, target):
        return pltpu.make_async_remote_copy(
            src_ref=src, dst_ref=dst, send_sem=send, recv_sem=recv,
            device_id={"pts": target}, device_id_type=pl.DeviceIdType.MESH,
        )

    def tri_copy(j):
        start = pl.multiple_of(j * size, size)
        return pltpu.make_async_copy(tri.at[:, pl.ds(start, size)], tbuf.at[j], t_sem.at[j])

    def each(count, fn):
        lax.fori_loop(0, count, lambda i, c: (fn(i), c)[1], 0)

    own_points = pltpu.make_async_copy(points, pbuf.at[chip], own_sem.at[0])
    own_centres = pltpu.make_async_copy(centres, cbuf.at[core], own_sem.at[1])
    own_points.start()
    own_centres.start()

    @functools.partial(each, n)
    def _(j):
        @pl.when(j >= me)
        def _():
            tri_copy(j).start()

    barrier = pltpu.get_barrier_semaphore()

    @functools.partial(each, n)
    def _(q):
        @pl.when(q != me)
        def _():
            pl.semaphore_signal(
                barrier, inc=1, device_id={"pts": q}, device_id_type=pl.DeviceIdType.MESH
            )

    pl.semaphore_wait(barrier, n - 1)

    def beta_send(q):
        return remote(beta, bbuf.at[me], b_send.at[q], b_recv.at[me], 2 * q + core)

    def beta_pass(q):
        block = 2 * q + core
        return remote(bbuf.at[block], bbuf.at[block], f_send.at[q], b_recv.at[block], partner)

    own_pass = remote(beta, bbuf.at[me], f_send.at[chip], b_recv.at[me], partner)
    centre_pass = remote(centres, cbuf.at[core], c_send, c_recv, partner)

    @functools.partial(each, chips)
    def _(q):
        @pl.when(q != chip)
        def _():
            beta_send(q).start()

    own_pass.start()
    centre_pass.start()
    bbuf[me] = beta[...]

    def chip_of(lev, sid):
        return 2 * lev + sid

    def point_copy(way, block):
        target = (chip + 2, chip - 2, chip_of(level, 1 - side))[way]
        return remote(
            pbuf.at[block], pbuf.at[block], p_send.at[way, block], p_recv.at[block],
            2 * target + core,
        )

    def point_sends(lev, act):
        block = chip_of(lev, side)
        for way, wanted in (
            (2, True),
            (0, (lev <= level) & (level < depth - 1)),
            (1, (lev >= level) & (level > 0)),
        ):
            @pl.when(wanted)
            def _():
                act(point_copy(way, block))

    own_points.wait()
    point_sends(level, lambda c: c.start())

    @functools.partial(each, chips)
    def _(q):
        @pl.when(q != chip)
        def _():
            remote(
                beta, bbuf.at[2 * q + core], b_send.at[q], b_recv.at[2 * q + core], partner
            ).wait_recv()
            beta_pass(q).start()

    own_centres.wait()
    remote(centres, cbuf.at[1 - core], c_send, c_recv, partner).wait_recv()

    def make_tile(block):
        for half in range(2):
            inner = dot(pbuf[block], cbuf[half], NT)
            value = inner * factor + 1.0
            kbuf[block, half] = (value * value * value).astype(jnp.bfloat16)

    make_tile(chip)

    @functools.partial(each, chips)
    def _(q):
        block = 2 * q + 1 - core
        remote(beta, bbuf.at[block], b_send.at[q], b_recv.at[block], partner).wait_recv()

    asum[...] = jnp.zeros_like(asum)

    def add_alpha(j):
        @pl.when((j >= me) & (j < n))
        def _():
            tri_copy(j).wait()
            asum[...] += dot(bbuf[j], tbuf[j], NT)

    def point_wait(block):
        remote(
            pbuf.at[block], pbuf.at[block], p_send.at[0, block], p_recv.at[block], partner
        ).wait_recv()

    share = -(-n // max(depth - 1, 1))

    def logit_copy(block):
        return remote(
            lsend.at[block], lrecv.at[chip], l_send.at[block], l_recv.at[chip], 2 * block + core
        )

    def logit_part(block):
        part = dot(abuf[0], kbuf[block, 0], NT) + dot(abuf[1], kbuf[block, 1], NT)

        @pl.when(block != chip)
        def _():
            lsend[block] = part
            logit_copy(block).start()

        @pl.when(block == chip)
        def _():
            lrecv[block] = part

    alpha_pass = remote(abuf.at[core], abuf.at[core], a_send, a_recv, partner)

    def step(d):
        for sign in (-1, 1):
            lev = level + sign * d

            @pl.when((lev >= 0) & (lev < depth))
            def _():
                point_wait(chip_of(lev, side))
                point_sends(lev, lambda c: c.start())

        each(share, lambda i: add_alpha((d - 1) * share + i))

        for sign in (-1, 1):
            lev = level + sign * d

            @pl.when((lev >= 0) & (lev < depth))
            def _():
                make_tile(chip_of(lev, side))

        def across(lev):
            @pl.when((lev >= 0) & (lev < depth))
            def _():
                point_wait(chip_of(lev, 1 - side))
                make_tile(chip_of(lev, 1 - side))

        across(level - d + 1)

        @pl.when(d > 1)
        def _():
            across(level + d - 1)

    each(depth - 1, lambda i: step(i + 1))
    abuf[core] = asum[...].astype(jnp.bfloat16)
    alpha_pass.start()
    remote(abuf.at[core], abuf.at[1 - core], a_send, a_recv, partner).wait_recv()

    def is_late(block):
        lev = block // 2
        far = (lev - level == depth - 1) | (level - lev == depth - 1)
        return far & (lax.rem(block, 2) != side)

    @functools.partial(each, chips)
    def _(block):
        @pl.when(jnp.logical_not(is_late(block)))
        def _():
            logit_part(block)

    @functools.partial(each, chips)
    def _(block):
        @pl.when(is_late(block))
        def _():
            point_wait(block)
            make_tile(block)
            logit_part(block)

    @functools.partial(each, chips)
    def _(q):
        @pl.when(q != chip)
        def _():
            remote(lsend.at[q], lrecv.at[q], l_send.at[q], l_recv.at[q], partner).wait_recv()

    logits = lrecv[0]
    for q in range(1, chips):
        logits = logits + lrecv[q]
    logits = logits + bias[...]
    logits_out[...] = logits
    onehot = (labels[...] == lax.broadcasted_iota(jnp.int32, logits.shape, 0)).astype(jnp.float32)
    rbuf[chip] = (jax.nn.sigmoid(logits) - onehot).astype(jnp.bfloat16)

    def resid_copy(q):
        return remote(rbuf.at[chip], rbuf.at[chip], r_send.at[q], r_recv.at[chip], 2 * q + core)

    @functools.partial(each, chips)
    def _(q):
        @pl.when(q != chip)
        def _():
            resid_copy(q).start()

    @functools.partial(each, chips)
    def _(q):
        @pl.when(q != chip)
        def _():
            remote(rbuf.at[q], rbuf.at[q], r_send.at[q], r_recv.at[q], partner).wait_recv()

    def grad_half(half):
        return lax.fori_loop(
            0, chips, lambda q, acc: acc + dot(rbuf[q], kbuf[q, half], NN),
            jnp.zeros((classes, size), jnp.float32),
        )

    gsend[...] = grad_half(1 - core)
    grad_pass = remote(gsend, grecv, g_send, g_recv, partner)
    grad_pass.start()
    mine = grad_half(core)
    grad_pass.wait_recv()
    coeff = ((mine + grecv[...]) * (1.0 / math.sqrt(total_points))).astype(jnp.bfloat16)

    def term_copy(j):
        return remote(tsend.at[j], trecv.at[me], ts_sem.at[j], tr_sem.at[me], j)

    @functools.partial(each, n)
    def _(i):
        j = n - 1 - i

        @pl.when(j >= me)
        def _():
            term = dot(coeff, tbuf[j], NN)

            @pl.when(j == me)
            def _():
                total[...] = term

            @pl.when(j != me)
            def _():
                tsend[j] = term.astype(tsend.dtype)
                term_copy(j).start()

    @functools.partial(each, n)
    def _(q):
        @pl.when(q < me)
        def _():
            remote(tsend.at[q], trecv.at[q], ts_sem.at[q], tr_sem.at[q], partner).wait_recv()
            total[...] += trecv[q].astype(jnp.float32)

    grad_out[...] = total[...]

    @functools.partial(each, chips)
    def _(q):
        @pl.when(q != chip)
        def _():
            beta_send(q).wait_send()
            beta_pass(q).wait_send()
            logit_copy(q).wait_send()
            resid_copy(q).wait_send()

    own_pass.wait_send()
    centre_pass.wait_send()
    alpha_pass.wait_send()
    grad_pass.wait_send()
    each(depth, lambda lev: point_sends(lev, lambda c: c.wait_send()))

    @functools.partial(each, n)
    def _(j):
        @pl.when(j > me)
        def _():
            term_copy(j).wait_send()


def on_device(points, labels, centres, tri_inverse, beta, bias):
    n = lax.axis_size("pts")
    chips = n // 2
    rows, features = points.shape
    size, classes = beta.shape
    low, full = jnp.bfloat16, jnp.float32
    dma = pltpu.SemaphoreType.DMA
    vmem = pl.BlockSpec(memory_space=pltpu.VMEM)
    hbm = pl.BlockSpec(memory_space=pl.ANY)
    grad_t, logits_t = pl.pallas_call(
        functools.partial(body, n),
        name="falkon_step",
        out_shape=(
            jax.ShapeDtypeStruct((classes, size), full),
            jax.ShapeDtypeStruct((classes, rows), full),
        ),
        in_specs=[hbm, vmem, hbm, hbm, vmem, vmem],
        out_specs=(vmem, vmem),
        scratch_shapes=[
            pltpu.VMEM((n, size, size), low),
            pltpu.VMEM((chips, rows, features), low),
            pltpu.VMEM((2, size, features), low),
            pltpu.VMEM((chips, 2, rows, size), low),
            pltpu.VMEM((n, classes, size), low),
            pltpu.VMEM((2, classes, size), low),
            pltpu.VMEM((classes, size), full),
            pltpu.VMEM((chips, classes, rows), full),
            pltpu.VMEM((chips, classes, rows), full),
            pltpu.VMEM((chips, classes, rows), low),
            pltpu.VMEM((classes, size), full),
            pltpu.VMEM((classes, size), full),
            pltpu.VMEM((n, classes, size), low),
            pltpu.VMEM((n, classes, size), low),
            pltpu.VMEM((classes, size), full),
            dma((n,)),
            dma((2,)),
            dma((chips,)),
            dma((n,)),
            dma((chips,)),
            dma((3, chips)),
            dma((chips,)),
            dma, dma, dma, dma,
            dma((chips,)),
            dma((chips,)),
            dma((chips,)),
            dma((chips,)),
            dma, dma,
            dma((n,)),
            dma((n,)),
        ],
        compiler_params=pltpu.CompilerParams(
            collective_id=0, has_side_effects=True, vmem_limit_bytes=60 * 1024 * 1024
        ),
    )(points, labels[None, :], centres, tri_inverse, beta.T, bias[:, None])
    return grad_t.T, logits_t.T


def solution(mesh):
    return jax.shard_map(
        on_device,
        mesh=mesh,
        in_specs=(
            P(("groups", "pts"), None),
            P(("groups", "pts")),
            P(("groups", "pts"), None),
            P(("groups", "pts"), None),
            P(("groups", "pts"), None),
            P("groups"),
        ),
        out_specs=(P(("groups", "pts"), None), P(("groups", "pts"), None)),
        check_vma=False,
    )
```

```python
import functools
import math

import jax
import jax.numpy as jnp
from jax import lax
from jax.experimental import pallas as pl
from jax.experimental.pallas import tpu as pltpu
from jax.sharding import PartitionSpec as P

NT = (((1,), (1,)), ((), ()))
NN = (((1,), (0,)), ((), ()))
PIECES = 4


def dot(left, right, dims):
    return lax.dot_general(left, right, dims, preferred_element_type=jnp.float32)


def body(
    n, points, labels, centres, tri, beta, bias, grad_out, logits_out,
    tbuf, pbuf, cbuf, kbuf, bbuf, abuf, asum, lsend, lrecv, rbuf, gsend, grecv, tsend, trecv, total,
    t_sem, own_sem, b_send, b_recv, f_send, p_send, p_recv, c_send, c_recv, a_send, a_recv,
    l_send, l_recv, r_send, r_recv, g_send, g_recv, ts_sem, tr_sem,
):
    chips = n // 2
    depth = chips // 2
    me = lax.axis_index("pts")
    core = lax.rem(me, 2)
    chip = me // 2
    side = lax.rem(chip, 2)
    level = chip // 2
    partner = me + 1 - 2 * core
    size = centres.shape[0]
    factor = 1.0 / math.sqrt(points.shape[1])
    total_points = n * points.shape[0]
    classes = beta.shape[0]

    def remote(src, dst, send, recv, target):
        return pltpu.make_async_remote_copy(
            src_ref=src, dst_ref=dst, send_sem=send, recv_sem=recv,
            device_id={"pts": target}, device_id_type=pl.DeviceIdType.MESH,
        )

    def tri_copy(j):
        start = pl.multiple_of(j * size, size)
        return pltpu.make_async_copy(tri.at[:, pl.ds(start, size)], tbuf.at[j], t_sem.at[j])

    def each(count, fn):
        lax.fori_loop(0, count, lambda i, c: (fn(i), c)[1], 0)

    own_points = pltpu.make_async_copy(points, pbuf.at[chip], own_sem.at[0])
    own_centres = pltpu.make_async_copy(centres, cbuf.at[core], own_sem.at[1])
    own_points.start()
    own_centres.start()

    @functools.partial(each, n)
    def _(j):
        @pl.when(j >= me)
        def _():
            tri_copy(j).start()

    barrier = pltpu.get_barrier_semaphore()

    @functools.partial(each, n)
    def _(q):
        @pl.when(q != me)
        def _():
            pl.semaphore_signal(
                barrier, inc=1, device_id={"pts": q}, device_id_type=pl.DeviceIdType.MESH
            )

    pl.semaphore_wait(barrier, n - 1)

    def beta_send(q):
        return remote(beta, bbuf.at[me], b_send.at[q], b_recv.at[me], 2 * q + core)

    def beta_pass(q):
        block = 2 * q + core
        return remote(bbuf.at[block], bbuf.at[block], f_send.at[q], b_recv.at[block], partner)

    own_pass = remote(beta, bbuf.at[me], f_send.at[chip], b_recv.at[me], partner)
    centre_pass = remote(centres, cbuf.at[core], c_send, c_recv, partner)

    @functools.partial(each, chips)
    def _(q):
        @pl.when(q < chip)
        def _():
            beta_send(q).start()

    own_pass.start()
    centre_pass.start()
    bbuf[me] = beta[...]

    def chip_of(lev, sid):
        return 2 * lev + sid

    piece_rows = points.shape[0] // PIECES

    def point_copy(way, block, piece):
        target = (chip + 2, chip - 2, chip_of(level, 1 - side))[way]
        rows = pbuf.at[block, pl.ds(piece * piece_rows, piece_rows)]
        return remote(
            rows, rows, p_send.at[way, block, piece], p_recv.at[block, piece], 2 * target + core
        )

    def point_sends(lev, piece, act):
        block = chip_of(lev, side)
        for way, wanted in (
            (0, (lev <= level) & (level < depth - 1)),
            (1, (lev >= level) & (level > 0)),
            (2, True),
        ):
            @pl.when(wanted)
            def _():
                act(point_copy(way, block, piece))

    own_points.wait()
    for piece in range(PIECES):
        point_sends(level, piece, lambda c: c.start())

    @functools.partial(each, chips)
    def _(q):
        @pl.when(q > chip)
        def _():
            remote(
                beta, bbuf.at[2 * q + core], b_send.at[q], b_recv.at[2 * q + core], partner
            ).wait_recv()
            beta_pass(q).start()

    own_centres.wait()
    remote(centres, cbuf.at[1 - core], c_send, c_recv, partner).wait_recv()

    def make_tile(block):
        for half in range(2):
            inner = dot(pbuf[block], cbuf[half], NT)
            value = inner * factor + 1.0
            kbuf[block, half] = (value * value * value).astype(jnp.bfloat16)

    make_tile(chip)

    @functools.partial(each, chips)
    def _(q):
        block = 2 * q + 1 - core

        @pl.when(q >= chip)
        def _():
            remote(beta, bbuf.at[block], b_send.at[q], b_recv.at[block], partner).wait_recv()

    asum[...] = jnp.zeros_like(asum)

    def add_alpha(j):
        @pl.when((j >= me) & (j < n))
        def _():
            tri_copy(j).wait()
            asum[...] += dot(bbuf[j], tbuf[j], NT)

    def piece_wait(block, piece):
        point_copy(2, block, piece).wait_recv()

    def point_wait(block):
        for piece in range(PIECES):
            piece_wait(block, piece)

    share = -(-n // max(depth - 1, 1))

    def logit_copy(block):
        return remote(
            lsend.at[block], lrecv.at[chip], l_send.at[block], l_recv.at[chip], 2 * block + core
        )

    def logit_part(block):
        part = dot(abuf[0], kbuf[block, 0], NT) + dot(abuf[1], kbuf[block, 1], NT)

        @pl.when(block != chip)
        def _():
            lsend[block] = part
            logit_copy(block).start()

        @pl.when(block == chip)
        def _():
            lrecv[block] = part

    alpha_pass = remote(abuf.at[core], abuf.at[core], a_send, a_recv, partner)

    def step(d):
        for piece in range(PIECES):
            for sign in (-1, 1):
                lev = level + sign * d

                @pl.when((lev >= 0) & (lev < depth))
                def _():
                    piece_wait(chip_of(lev, side), piece)
                    point_sends(lev, piece, lambda c: c.start())

            first = piece * share // PIECES
            count = (piece + 1) * share // PIECES - first
            each(count, lambda i: add_alpha((d - 1) * share + first + i))

        for sign in (-1, 1):
            lev = level + sign * d

            @pl.when((lev >= 0) & (lev < depth))
            def _():
                make_tile(chip_of(lev, side))

        def across(lev):
            @pl.when((lev >= 0) & (lev < depth))
            def _():
                point_wait(chip_of(lev, 1 - side))
                make_tile(chip_of(lev, 1 - side))

        across(level - d + 1)

        @pl.when(d > 1)
        def _():
            across(level + d - 1)

    each(depth - 1, lambda i: step(i + 1))
    abuf[core] = asum[...].astype(jnp.bfloat16)
    alpha_pass.start()
    remote(abuf.at[core], abuf.at[1 - core], a_send, a_recv, partner).wait_recv()

    def is_late(block):
        lev = block // 2
        far = (lev - level == depth - 1) | (level - lev == depth - 1)
        return far & (lax.rem(block, 2) != side)

    @functools.partial(each, chips)
    def _(block):
        @pl.when(jnp.logical_not(is_late(block)))
        def _():
            logit_part(block)

    @functools.partial(each, chips)
    def _(block):
        @pl.when(is_late(block))
        def _():
            point_wait(block)
            make_tile(block)
            logit_part(block)

    @functools.partial(each, chips)
    def _(q):
        @pl.when(q != chip)
        def _():
            remote(lsend.at[q], lrecv.at[q], l_send.at[q], l_recv.at[q], partner).wait_recv()

    logits = lrecv[0]
    for q in range(1, chips):
        logits = logits + lrecv[q]
    spot = lax.broadcasted_iota(jnp.int32, (classes, classes), 0)
    other = lax.broadcasted_iota(jnp.int32, (classes, classes), 1)
    row = jnp.broadcast_to(bias[...], (classes, classes))
    column = jnp.sum(jnp.where(spot == other, row, 0.0), axis=1, keepdims=True)
    logits = logits + column
    logits_out[...] = logits
    onehot = (labels[...] == lax.broadcasted_iota(jnp.int32, logits.shape, 0)).astype(jnp.float32)
    rbuf[chip] = (jax.nn.sigmoid(logits) - onehot).astype(jnp.bfloat16)

    def resid_copy(q):
        return remote(rbuf.at[chip], rbuf.at[chip], r_send.at[q], r_recv.at[chip], 2 * q + core)

    @functools.partial(each, chips)
    def _(q):
        @pl.when(q != chip)
        def _():
            resid_copy(q).start()

    @functools.partial(each, chips)
    def _(q):
        @pl.when(q != chip)
        def _():
            remote(rbuf.at[q], rbuf.at[q], r_send.at[q], r_recv.at[q], partner).wait_recv()

    def grad_half(half):
        return lax.fori_loop(
            0, chips, lambda q, acc: acc + dot(rbuf[q], kbuf[q, half], NN),
            jnp.zeros((classes, size), jnp.float32),
        )

    gsend[...] = grad_half(1 - core)
    grad_pass = remote(gsend, grecv, g_send, g_recv, partner)
    grad_pass.start()
    mine = grad_half(core)
    grad_pass.wait_recv()
    coeff = ((mine + grecv[...]) * (1.0 / math.sqrt(total_points))).astype(jnp.bfloat16)

    def term_copy(j):
        return remote(tsend.at[j], trecv.at[me], ts_sem.at[j], tr_sem.at[me], j)

    @functools.partial(each, n)
    def _(i):
        j = n - 1 - i

        @pl.when(j >= me)
        def _():
            term = dot(coeff, tbuf[j], NN)

            @pl.when(j == me)
            def _():
                total[...] = term

            @pl.when(j != me)
            def _():
                tsend[j] = term.astype(tsend.dtype)
                term_copy(j).start()

    @functools.partial(each, n)
    def _(q):
        @pl.when(q < me)
        def _():
            remote(tsend.at[q], trecv.at[q], ts_sem.at[q], tr_sem.at[q], partner).wait_recv()
            total[...] += trecv[q].astype(jnp.float32)

    grad_out[...] = total[...]

    @functools.partial(each, chips)
    def _(q):
        @pl.when(q < chip)
        def _():
            beta_send(q).wait_send()

        @pl.when(q > chip)
        def _():
            beta_pass(q).wait_send()

        @pl.when(q != chip)
        def _():
            logit_copy(q).wait_send()
            resid_copy(q).wait_send()

    own_pass.wait_send()
    centre_pass.wait_send()
    alpha_pass.wait_send()
    grad_pass.wait_send()
    for piece in range(PIECES):
        each(depth, lambda lev: point_sends(lev, piece, lambda c: c.wait_send()))

    @functools.partial(each, n)
    def _(j):
        @pl.when(j > me)
        def _():
            term_copy(j).wait_send()


def write_out(grad, logits, grad_out, logits_out):
    grad_out[...] = grad[...]
    logits_out[...] = logits[...]


def on_device(points, labels, centres, tri_inverse, beta, bias):
    n = lax.axis_size("pts")
    chips = n // 2
    rows, features = points.shape
    size, classes = beta.shape
    low, full = jnp.bfloat16, jnp.float32
    dma = pltpu.SemaphoreType.DMA
    vmem = pl.BlockSpec(memory_space=pltpu.VMEM)
    hbm = pl.BlockSpec(memory_space=pl.ANY)
    grad_t, logits_t = pl.pallas_call(
        functools.partial(body, n),
        name="falkon_step",
        out_shape=(
            jax.ShapeDtypeStruct((classes, size), full),
            jax.ShapeDtypeStruct((classes, rows), full),
        ),
        in_specs=[hbm, vmem, hbm, hbm, vmem, vmem],
        out_specs=(vmem, vmem),
        scratch_shapes=[
            pltpu.VMEM((n, size, size), low),
            pltpu.VMEM((chips, rows, features), low),
            pltpu.VMEM((2, size, features), low),
            pltpu.VMEM((chips, 2, rows, size), low),
            pltpu.VMEM((n, classes, size), low),
            pltpu.VMEM((2, classes, size), low),
            pltpu.VMEM((classes, size), full),
            pltpu.VMEM((chips, classes, rows), full),
            pltpu.VMEM((chips, classes, rows), full),
            pltpu.VMEM((chips, classes, rows), low),
            pltpu.VMEM((classes, size), full),
            pltpu.VMEM((classes, size), full),
            pltpu.VMEM((n, classes, size), low),
            pltpu.VMEM((n, classes, size), low),
            pltpu.VMEM((classes, size), full),
            dma((n,)),
            dma((2,)),
            dma((chips,)),
            dma((n,)),
            dma((chips,)),
            dma((3, chips, PIECES)),
            dma((chips, PIECES)),
            dma, dma, dma, dma,
            dma((chips,)),
            dma((chips,)),
            dma((chips,)),
            dma((chips,)),
            dma, dma,
            dma((n,)),
            dma((n,)),
        ],
        compiler_params=pltpu.CompilerParams(
            collective_id=0, has_side_effects=True, vmem_limit_bytes=60 * 1024 * 1024
        ),
    )(points, labels[None, :], centres, tri_inverse, beta.T, bias[None, :])
    grad_t, logits_t = pl.pallas_call(
        write_out,
        name="write_out",
        out_shape=(
            jax.ShapeDtypeStruct(grad_t.shape, full),
            jax.ShapeDtypeStruct(logits_t.shape, full),
        ),
        in_specs=[vmem, vmem],
        out_specs=(vmem, vmem),
    )(grad_t, logits_t)
    return grad_t.T, logits_t.T


def solution(mesh):
    return jax.shard_map(
        on_device,
        mesh=mesh,
        in_specs=(
            P(("groups", "pts"), None),
            P(("groups", "pts")),
            P(("groups", "pts"), None),
            P(("groups", "pts"), None),
            P(("groups", "pts"), None),
            P("groups"),
        ),
        out_specs=(P(("groups", "pts"), None), P(("groups", "pts"), None)),
        check_vma=False,
    )
```

```python
import functools
import math

import jax
import jax.numpy as jnp
from jax import lax
from jax.experimental import pallas as pl
from jax.experimental.pallas import tpu as pltpu
from jax.sharding import PartitionSpec as P

NT = (((1,), (1,)), ((), ()))
NN = (((1,), (0,)), ((), ()))
PIECES = 4


def dot(left, right, dims):
    return lax.dot_general(left, right, dims, preferred_element_type=jnp.float32)


def body(
    n, points, labels, centres, tri, beta, bias, grad_out, logits_out,
    tbuf, pbuf, cbuf, kbuf, bbuf, abuf, asum, lsend, lrecv, rbuf, gsend, grecv, tsend, trecv, total, xsend, xrecv, xown,
    t_sem, own_sem, b_send, b_recv, f_send, p_send, p_recv, c_send, c_recv, a_send, a_recv,
    l_send, l_recv, r_send, r_recv, g_send, g_recv, ts_sem, tr_sem, xs_sem, xr_sem,
):
    chips = n // 2
    depth = chips // 2
    me = lax.axis_index("pts")
    core = lax.rem(me, 2)
    chip = me // 2
    side = lax.rem(chip, 2)
    level = chip // 2
    partner = me + 1 - 2 * core
    size = centres.shape[0]
    factor = 1.0 / math.sqrt(points.shape[1])
    total_points = n * points.shape[0]
    classes = beta.shape[0]

    def remote(src, dst, send, recv, target):
        return pltpu.make_async_remote_copy(
            src_ref=src, dst_ref=dst, send_sem=send, recv_sem=recv,
            device_id={"pts": target}, device_id_type=pl.DeviceIdType.MESH,
        )

    def tri_copy(j):
        start = pl.multiple_of(j * size, size)
        return pltpu.make_async_copy(tri.at[:, pl.ds(start, size)], tbuf.at[j], t_sem.at[j])

    def each(count, fn):
        lax.fori_loop(0, count, lambda i, c: (fn(i), c)[1], 0)

    own_points = pltpu.make_async_copy(points, pbuf.at[chip], own_sem.at[0])
    own_centres = pltpu.make_async_copy(centres, cbuf.at[core], own_sem.at[1])
    own_points.start()
    own_centres.start()

    @functools.partial(each, n)
    def _(j):
        @pl.when(j >= me)
        def _():
            tri_copy(j).start()

    barrier = pltpu.get_barrier_semaphore()

    @functools.partial(each, n)
    def _(q):
        @pl.when(q != me)
        def _():
            pl.semaphore_signal(
                barrier, inc=1, device_id={"pts": q}, device_id_type=pl.DeviceIdType.MESH
            )

    pl.semaphore_wait(barrier, n - 1)

    def beta_send(q):
        return remote(beta, bbuf.at[me], b_send.at[q], b_recv.at[me], 2 * q + core)

    def beta_pass(q):
        block = 2 * q + core
        return remote(bbuf.at[block], bbuf.at[block], f_send.at[q], b_recv.at[block], partner)

    own_pass = remote(beta, bbuf.at[me], f_send.at[chip], b_recv.at[me], partner)
    centre_pass = remote(centres, cbuf.at[core], c_send, c_recv, partner)

    @functools.partial(each, chips)
    def _(q):
        @pl.when(q < chip)
        def _():
            beta_send(q).start()

    own_pass.start()
    centre_pass.start()
    bbuf[me] = beta[...]

    def chip_of(lev, sid):
        return 2 * lev + sid

    piece_rows = points.shape[0] // PIECES

    def point_copy(way, block, piece):
        target = (chip + 2, chip - 2, chip_of(level, 1 - side))[way]
        rows = pbuf.at[block, pl.ds(piece * piece_rows, piece_rows)]
        return remote(
            rows, rows, p_send.at[way, block, piece], p_recv.at[block, piece], 2 * target + core
        )

    def point_sends(lev, piece, act):
        block = chip_of(lev, side)
        for way, wanted in (
            (0, (lev <= level) & (level < depth - 1)),
            (1, (lev >= level) & (level > 0)),
            (2, True),
        ):
            @pl.when(wanted)
            def _():
                act(point_copy(way, block, piece))

    own_points.wait()
    for piece in range(PIECES):
        point_sends(level, piece, lambda c: c.start())

    @functools.partial(each, chips)
    def _(q):
        @pl.when(q > chip)
        def _():
            remote(
                beta, bbuf.at[2 * q + core], b_send.at[q], b_recv.at[2 * q + core], partner
            ).wait_recv()
            beta_pass(q).start()

    own_centres.wait()
    remote(centres, cbuf.at[1 - core], c_send, c_recv, partner).wait_recv()

    def make_tile(block):
        for half in range(2):
            inner = dot(pbuf[block], cbuf[half], NT)
            value = inner * factor + 1.0
            kbuf[block, half] = (value * value * value).astype(jnp.bfloat16)

    make_tile(chip)

    @functools.partial(each, chips)
    def _(q):
        block = 2 * q + 1 - core

        @pl.when(q >= chip)
        def _():
            remote(beta, bbuf.at[block], b_send.at[q], b_recv.at[block], partner).wait_recv()

    asum[...] = jnp.zeros_like(asum)

    def add_alpha(j):
        @pl.when((j >= me) & (j < n))
        def _():
            tri_copy(j).wait()
            asum[...] += dot(bbuf[j], tbuf[j], NT)

    def piece_wait(block, piece):
        point_copy(2, block, piece).wait_recv()

    def point_wait(block):
        for piece in range(PIECES):
            piece_wait(block, piece)

    share = -(-n // max(depth - 1, 1))

    def logit_copy(block):
        return remote(
            lsend.at[block], lrecv.at[chip], l_send.at[block], l_recv.at[chip], 2 * block + core
        )

    def logit_part(block):
        part = dot(abuf[0], kbuf[block, 0], NT) + dot(abuf[1], kbuf[block, 1], NT)

        @pl.when(block != chip)
        def _():
            lsend[block] = part
            logit_copy(block).start()

        @pl.when(block == chip)
        def _():
            lrecv[block] = part

    alpha_pass = remote(abuf.at[core], abuf.at[core], a_send, a_recv, partner)

    def step(d):
        for piece in range(PIECES):
            for sign in (-1, 1):
                lev = level + sign * d

                @pl.when((lev >= 0) & (lev < depth))
                def _():
                    piece_wait(chip_of(lev, side), piece)
                    point_sends(lev, piece, lambda c: c.start())

            first = piece * share // PIECES
            count = (piece + 1) * share // PIECES - first
            each(count, lambda i: add_alpha((d - 1) * share + first + i))

        for sign in (-1, 1):
            lev = level + sign * d

            @pl.when((lev >= 0) & (lev < depth))
            def _():
                make_tile(chip_of(lev, side))

        def across(lev):
            @pl.when((lev >= 0) & (lev < depth))
            def _():
                point_wait(chip_of(lev, 1 - side))
                make_tile(chip_of(lev, 1 - side))

        across(level - d + 1)

        @pl.when(d > 1)
        def _():
            across(level + d - 1)

    each(depth - 1, lambda i: step(i + 1))
    abuf[core] = asum[...].astype(jnp.bfloat16)
    alpha_pass.start()
    remote(abuf.at[core], abuf.at[1 - core], a_send, a_recv, partner).wait_recv()

    def is_late(block):
        lev = block // 2
        far = (lev - level == depth - 1) | (level - lev == depth - 1)
        return far & (lax.rem(block, 2) != side)

    @functools.partial(each, chips)
    def _(block):
        @pl.when(jnp.logical_not(is_late(block)))
        def _():
            logit_part(block)

    @functools.partial(each, chips)
    def _(block):
        @pl.when(is_late(block))
        def _():
            point_wait(block)
            make_tile(block)
            logit_part(block)

    @functools.partial(each, chips)
    def _(q):
        @pl.when(q != chip)
        def _():
            remote(lsend.at[q], lrecv.at[q], l_send.at[q], l_recv.at[q], partner).wait_recv()

    logits = lrecv[0]
    for q in range(1, chips):
        logits = logits + lrecv[q]
    spot = lax.broadcasted_iota(jnp.int32, (classes, classes), 0)
    other = lax.broadcasted_iota(jnp.int32, (classes, classes), 1)
    row = jnp.broadcast_to(bias[...], (classes, classes))
    column = jnp.sum(jnp.where(spot == other, row, 0.0), axis=1, keepdims=True)
    logits = logits + column
    logits_out[...] = logits
    onehot = (labels[...] == lax.broadcasted_iota(jnp.int32, logits.shape, 0)).astype(jnp.float32)
    rbuf[chip] = (jax.nn.sigmoid(logits) - onehot).astype(jnp.bfloat16)

    def resid_copy(q):
        return remote(rbuf.at[chip], rbuf.at[chip], r_send.at[q], r_recv.at[chip], 2 * q + core)

    @functools.partial(each, chips)
    def _(q):
        @pl.when(q != chip)
        def _():
            resid_copy(q).start()

    @functools.partial(each, chips)
    def _(q):
        @pl.when(q != chip)
        def _():
            remote(rbuf.at[q], rbuf.at[q], r_send.at[q], r_recv.at[q], partner).wait_recv()

    def grad_half(half):
        return lax.fori_loop(
            0, chips, lambda q, acc: acc + dot(rbuf[q], kbuf[q, half], NN),
            jnp.zeros((classes, size), jnp.float32),
        )

    gsend[...] = grad_half(1 - core)
    grad_pass = remote(gsend, grecv, g_send, g_recv, partner)
    grad_pass.start()
    mine = grad_half(core)
    grad_pass.wait_recv()
    coeff = ((mine + grecv[...]) * (1.0 / math.sqrt(total_points))).astype(jnp.bfloat16)

    def term_copy(q):
        return remote(tsend.at[q], trecv.at[chip], ts_sem.at[q], tr_sem.at[chip], 2 * q + core)

    def pair_copy(q):
        return remote(xsend.at[q], xrecv.at[q], xs_sem.at[q], xr_sem.at[q], partner)

    def to_pair(q):
        return (q > chip) | ((q == chip) & (core == 0))

    def finish(q):
        pair_copy(q).wait_recv()
        tsend[q] = (xown[q] + xrecv[q]).astype(tsend.dtype)
        term_copy(q).start()

    @functools.partial(each, chips)
    def _(i):
        q = chips - 1 - i

        @pl.when(to_pair(q))
        def _():
            xsend[q] = dot(coeff, tbuf[2 * q + 1 - core], NN)
            pair_copy(q).start()

        @pl.when(q >= chip)
        def _():
            xown[q] = dot(coeff, tbuf[2 * q + core], NN)

        @pl.when((q >= chip) & (q + 1 < chips))
        def _():
            finish(q + 1)

    total[...] = xown[chip]

    @pl.when(core == 1)
    def _():
        pair_copy(chip).wait_recv()
        total[...] += xrecv[chip]

    @functools.partial(each, chips)
    def _(q):
        @pl.when(q < chip)
        def _():
            remote(tsend.at[q], trecv.at[q], ts_sem.at[q], tr_sem.at[q], partner).wait_recv()
            total[...] += trecv[q].astype(jnp.float32)

    grad_out[...] = total[...]

    @functools.partial(each, chips)
    def _(q):
        @pl.when(q < chip)
        def _():
            beta_send(q).wait_send()

        @pl.when(q > chip)
        def _():
            beta_pass(q).wait_send()

        @pl.when(q != chip)
        def _():
            logit_copy(q).wait_send()
            resid_copy(q).wait_send()

    own_pass.wait_send()
    centre_pass.wait_send()
    alpha_pass.wait_send()
    grad_pass.wait_send()
    for piece in range(PIECES):
        each(depth, lambda lev: point_sends(lev, piece, lambda c: c.wait_send()))

    @functools.partial(each, chips)
    def _(q):
        @pl.when(to_pair(q))
        def _():
            pair_copy(q).wait_send()

        @pl.when(q > chip)
        def _():
            term_copy(q).wait_send()


def write_out(grad, logits, grad_out, logits_out):
    grad_out[...] = grad[...]
    logits_out[...] = logits[...]


def on_device(points, labels, centres, tri_inverse, beta, bias):
    n = lax.axis_size("pts")
    chips = n // 2
    rows, features = points.shape
    size, classes = beta.shape
    low, full = jnp.bfloat16, jnp.float32
    dma = pltpu.SemaphoreType.DMA
    vmem = pl.BlockSpec(memory_space=pltpu.VMEM)
    hbm = pl.BlockSpec(memory_space=pl.ANY)
    grad_t, logits_t = pl.pallas_call(
        functools.partial(body, n),
        name="falkon_step",
        out_shape=(
            jax.ShapeDtypeStruct((classes, size), full),
            jax.ShapeDtypeStruct((classes, rows), full),
        ),
        in_specs=[hbm, vmem, hbm, hbm, vmem, vmem],
        out_specs=(vmem, vmem),
        scratch_shapes=[
            pltpu.VMEM((n, size, size), low),
            pltpu.VMEM((chips, rows, features), low),
            pltpu.VMEM((2, size, features), low),
            pltpu.VMEM((chips, 2, rows, size), low),
            pltpu.VMEM((n, classes, size), low),
            pltpu.VMEM((2, classes, size), low),
            pltpu.VMEM((classes, size), full),
            pltpu.VMEM((chips, classes, rows), full),
            pltpu.VMEM((chips, classes, rows), full),
            pltpu.VMEM((chips, classes, rows), low),
            pltpu.VMEM((classes, size), full),
            pltpu.VMEM((classes, size), full),
            pltpu.VMEM((chips, classes, size), low),
            pltpu.VMEM((chips, classes, size), low),
            pltpu.VMEM((classes, size), full),
            pltpu.VMEM((chips, classes, size), full),
            pltpu.VMEM((chips, classes, size), full),
            pltpu.VMEM((chips, classes, size), full),
            dma((n,)),
            dma((2,)),
            dma((chips,)),
            dma((n,)),
            dma((chips,)),
            dma((3, chips, PIECES)),
            dma((chips, PIECES)),
            dma, dma, dma, dma,
            dma((chips,)),
            dma((chips,)),
            dma((chips,)),
            dma((chips,)),
            dma, dma,
            dma((chips,)),
            dma((chips,)),
            dma((chips,)),
            dma((chips,)),
        ],
        compiler_params=pltpu.CompilerParams(
            collective_id=0, has_side_effects=True, vmem_limit_bytes=60 * 1024 * 1024
        ),
    )(points, labels[None, :], centres, tri_inverse, beta.T, bias[None, :])
    grad_t, logits_t = pl.pallas_call(
        write_out,
        name="write_out",
        out_shape=(
            jax.ShapeDtypeStruct(grad_t.shape, full),
            jax.ShapeDtypeStruct(logits_t.shape, full),
        ),
        in_specs=[vmem, vmem],
        out_specs=(vmem, vmem),
    )(grad_t, logits_t)
    return grad_t.T, logits_t.T


def solution(mesh):
    return jax.shard_map(
        on_device,
        mesh=mesh,
        in_specs=(
            P(("groups", "pts"), None),
            P(("groups", "pts")),
            P(("groups", "pts"), None),
            P(("groups", "pts"), None),
            P(("groups", "pts"), None),
            P("groups"),
        ),
        out_specs=(P(("groups", "pts"), None), P(("groups", "pts"), None)),
        check_vma=False,
    )
```
